32 devices in a mesh: pipe: 2 (over x), expert: 4 (over y, core), tensor: 4 (over z).
Axes of the slice: x: 2, y: 2, z: 4, core: 2. Of those that a mesh axis runs over, the one named last changes fastest.
Arguments:
- inputs: bfloat16 [2, 1152, 768], P(None, ('expert', 'tensor')), may hold values from -6 to 6
- cotangent: bfloat16 [2, 1152, 768], P(None, ('expert', 'tensor')), may hold values from -6 to 6
- qkv_weight: bfloat16 [2, 768, 3, 768], P('pipe', None, None, 'tensor'), may hold values from -0.21875 to 0.21875
- out_weight: bfloat16 [2, 768, 768], P('pipe', 'tensor'), may hold values from -2.5 to 2.5
- rel_bias: bfloat16 [2, 32, 12], P('pipe', None, 'tensor'), may hold values from -4 to 4
- norm_gains: bfloat16 [2, 2, 768], P('pipe'), may hold values from 0.099609375 to 1.8984375
- first_weight: bfloat16 [2, 8, 768, 3072], P('pipe', 'expert', None, 'tensor'), may hold values from -0.21875 to 0.21875
- second_weight: bfloat16 [2, 8, 3072, 768], P('pipe', 'expert', 'tensor'), may hold values from -0.109375 to 0.109375
- routes: int32 [2, 2, 1152, 2], P('pipe', None, 'expert'), may hold values from 0 to 7, all different within a row; in each aligned block of 288 rows (0 to 287, 288 to 575, ..., all dimensions but the last counted through in order) at most 144 rows name the same one
- gates: float32 [2, 2, 1152, 2], P('pipe', None, 'expert'), may hold values from 0.1 to 1
- piece_starts: int32 [2, 4], P(None, 'expert'), may hold values from 0 to 32
Outputs:
- activations: bfloat16 [2, 2, 1152, 768], P('pipe', None, ('expert', 'tensor'))
- input_grads: bfloat16 [2, 2, 1152, 768], P('pipe', None, ('expert', 'tensor'))
- qkv_grad: float32 [2, 768, 3, 768], P('pipe', None, None, 'tensor')
- out_grad: float32 [2, 768, 768], P('pipe', 'tensor')
- bias_grad: float32 [2, 32, 12], P('pipe', None, 'tensor')
- gain_grad: float32 [2, 2, 768], P('pipe')
- first_grad: float32 [2, 8, 768, 3072], P('pipe', 'expert', None, 'tensor')
- second_grad: float32 [2, 8, 3072, 768], P('pipe', 'expert', 'tensor')
The draws below stay inside these ranges and needn't reach their ends.
Inputs may be any that keep to these rules, and one draw needn't show every extreme that they name: `routes`: each token names 2 different experts. Among the 288 tokens of one sequence in one micro-batch and layer no expert is named more than 144 times, and in some such sequence an expert is named exactly 144 times. `piece_starts`: the picture piece of a sequence is the 256 positions from its start.
All inputs are finite; a program needn't handle non-finite values.
Results may differ from the reference program's by a relative error of at most 0.03.
Values may be sent and summed in bfloat16 or wider, within the bound.
No kernel may reach another device: no remote copies, remote signals or barrier semaphores. Data moves between devices by JAX's collectives and lax.ppermute only.
A program may use at most 192 MiB of HBM per device.

```python
import math
import jax
import jax.numpy as jnp
import numpy as np
from jax import lax

D = 768
HEADS = 12
DH = 64
FF = 3072
TOP = 2
NB = 32
PIECE = 256
MICRO = 2
SEQ = 288
LAYERS = 2
EXPERTS = 8
CAP = 144
TOKENS_MB = 1152
N_EXPERT = 4


def plant(array, stream_key, smallest, top_value):
    longest = array.shape.index(max(array.shape))
    spots = []
    for shift in (0, 1):
        where = [jax.random.randint(jax.random.fold_in(stream_key, axis), (), 0, length) for axis, length in enumerate(array.shape)]
        where[longest] = (where[longest] + shift) % array.shape[longest]
        spots.append(tuple(where))
    return array.at[spots[0]].set(smallest).at[spots[1]].set(top_value)


def levels(rng, dims, shards, smallest, largest):
    gain, own = 1.0, jax.random.fold_in(rng, 6)
    for dim, shards_of in shards:
        steps = jnp.exp(jax.random.uniform(jax.random.fold_in(own, dim), (shards_of,), jnp.float32, smallest / len(shards), largest / len(shards)))
        gain = gain * jnp.repeat(steps, dims[dim] // shards_of).reshape([-1 if axis == dim else 1 for axis in range(len(dims))])
    return gain


def assign_block(own_key, own, number, rows, count, top, bound, slope):
    ranking = jax.random.permutation(own_key, count)
    heavy_load, ordinary = load_shares(count, rows * top, bound, slope, True), load_shares(count, rows * top, bound, slope, False)
    places = jnp.arange(count)

    def named(sizes, turn):
        used = int((sizes > 0).sum())
        fixed = max(1, used // 4)
        passed = fixed + (places - fixed + turn * (used - fixed)) % max(1, count - fixed)
        return jnp.zeros((count,), jnp.int32).at[ranking[jnp.where(places < fixed, places, passed)]].set(jnp.asarray(sizes, jnp.int32))

    sizes = jnp.where(number % 4 == 0, named(heavy_load, number // 4), named(ordinary, number - number // 4 - 1))
    mixed = jax.random.permutation(jax.random.fold_in(own, 3), count)
    source_of, taker = mixed[0:count // 2 * 2:2], mixed[1:count // 2 * 2:2]
    margin = jnp.minimum(sizes[source_of] - 1, bound - sizes[taker]) // 2
    margin = jnp.where((source_of == ranking[0]) | (taker == ranking[0]) | (sizes[taker] == 0), 0, jnp.maximum(margin, 0))
    passed = jax.random.randint(jax.random.fold_in(own, 4), (count // 2,), 0, 1 << 20) % (margin + 1)
    sizes = sizes.at[source_of].add(-passed).at[taker].add(passed)
    members = jnp.searchsorted(jnp.cumsum(sizes), jnp.arange(rows * top), side="right").astype(jnp.int32)
    grid = members.reshape(top, rows).T
    grid = grid[jax.random.permutation(jax.random.fold_in(own, 1), rows)]
    turn = jax.random.randint(jax.random.fold_in(own, 2), (rows, 1), 0, top)
    return jnp.take_along_axis(grid, (jnp.arange(top)[None, :] + turn) % top, axis=1)


def load_shares(number_of, total, bound, slope, full):
    weights = [(1 << 20) // math.isqrt(grade ** slope) + 1 for grade in range(1, number_of + 1)]
    largest = bound if full else min(bound, max(-(-total // number_of), total * weights[0] // sum(weights)))
    least = 1 if total - largest >= number_of - 1 else 0
    given, surplus = [largest] + [least] * (number_of - 1), total - largest - least * (number_of - 1)
    while surplus > 0:
        candidates = [i for i in range(1, number_of) if given[i] < largest] or [i for i in range(1, number_of) if given[i] < bound]
        mass, left = sum([weights[i] for i in candidates]), surplus
        for i in candidates:
            more = min(bound - given[i], max(1, left * weights[i] // mass), surplus)
            given[i] = given[i] + more
            surplus = surplus - more
    return np.array(given)


def gaussian(key, dims, spread, reach, pieces=(), kind=jnp.bfloat16):
    drawn = spread * jax.random.normal(key, dims, jnp.float32)
    if pieces:
        drawn = drawn * levels(key, dims, pieces, -0.22, 0.18)
    return jnp.clip(drawn, -reach, reach).astype(kind)


def setup_inputs(seed: int = 0) -> dict:
    splits = jax.random.split(jax.random.key(seed), 12)
    inputs = gaussian(splits[0], (MICRO, TOKENS_MB, D), 1.0, 6.0, ((1, 16),))
    cotangent = gaussian(splits[1], (MICRO, TOKENS_MB, D), 1.0, 6.0, ((1, 16),))
    qkv_weight = gaussian(splits[2], (LAYERS, D, 3, HEADS * DH), D ** -0.5, 0.21875, ((0, 2), (3, 4)))
    out_weight = gaussian(splits[3], (LAYERS, HEADS * DH, D), (max(HEADS * DH // 128, 1)) ** -0.5, 2.5, ((0, 2), (1, 4)))
    rel_bias = gaussian(splits[4], (LAYERS, NB, HEADS), 1.0, 4.0, ((0, 2), (2, 4)))
    norm_gains = jnp.clip(1.0 + 0.18 * jax.random.normal(splits[5], (LAYERS, 2, D), jnp.float32), 0.099609375, 1.8984375).astype(jnp.bfloat16)
    first_weight = gaussian(splits[6], (LAYERS, EXPERTS, D, FF), D ** -0.5, 0.21875, ((0, 2), (1, 4), (3, 4)))
    second_weight = gaussian(splits[7], (LAYERS, EXPERTS, FF, D), FF ** -0.5, 0.109375, ((0, 2), (1, 4), (2, 4)))
    routes_keys = jax.random.split(jax.random.fold_in(splits[8], 1), LAYERS * MICRO * TOKENS_MB // SEQ)
    routes_turns = jax.random.permutation(jax.random.fold_in(splits[8], 3), LAYERS * MICRO * TOKENS_MB // SEQ)
    routes = jax.vmap(lambda own, number: assign_block(jax.random.fold_in(splits[8], 2), own, number, SEQ, EXPERTS, TOP, CAP, 1))(routes_keys, routes_turns).reshape((LAYERS, MICRO, TOKENS_MB, TOP))
    gates = jnp.clip(0.1 + 0.9 * jax.random.uniform(splits[9], (LAYERS, MICRO, TOKENS_MB, TOP), jnp.float32) ** levels(splits[9], (LAYERS, MICRO, TOKENS_MB, TOP), ((0, 2), (2, 4)), -0.2, 0.2), 0.1, 1.0)
    piece_starts = plant(jax.random.randint(splits[10], (MICRO, N_EXPERT), 0, SEQ - PIECE + 1), jax.random.fold_in(splits[10], 1), 0, SEQ - PIECE).astype(jnp.int32)
    return {"inputs": inputs, "cotangent": cotangent, "qkv_weight": qkv_weight, "out_weight": out_weight, "rel_bias": rel_bias, "norm_gains": norm_gains, "first_weight": first_weight, "second_weight": second_weight, "routes": routes, "gates": gates, "piece_starts": piece_starts}


@jax.custom_vjp
def low(v):
    return lax.optimization_barrier(v.astype(jnp.bfloat16)).astype(jnp.float32)

@jax.custom_vjp
def low_back(v):
    return v

def low_keep(v):
    return (low(v), None)

def low_pass(kept, grad):
    return (grad,)

def back_keep(v):
    return (v, None)

def back_low(kept, grad):
    return (low(grad),)
low.defvjp(low_keep, low_pass)
low_back.defvjp(back_keep, back_low)
EPSILON = 1e-06
PRECISE = lax.Precision.HIGHEST

def rms_norm(values, gain_values):
    return values * lax.rsqrt(lax.optimization_barrier(jnp.mean(values * values, axis=-1, keepdims=True)) + EPSILON) * gain_values

def bucket_of(offset):
    half_count = NB // 2
    magnitude = jnp.abs(offset)
    octave = jnp.zeros_like(magnitude)
    for exponent in range(1, 13):
        octave = octave + (magnitude >= 2 ** exponent).astype(jnp.int32)
    inside_bucket = jnp.where(magnitude < 8, magnitude, jnp.minimum(5 + octave, half_count - 1))
    return inside_bucket + half_count * (offset > 0).astype(jnp.int32)

def bias_onehot(length):
    positions = jnp.arange(length, dtype=jnp.int32)
    offsets = positions[None, :] - positions[:, None]
    buckets = bucket_of(offsets)
    return (buckets[:, :, None] == jnp.arange(NB, dtype=jnp.int32)).astype(jnp.float32)

def attend_group(qkv_group, starts_group, position_bias):
    queries = qkv_group[:, :, 0]
    keys_all = qkv_group[:, :, 1]
    values_all = qkv_group[:, :, 2]
    products = jnp.einsum('gihd,gjhd->ghij', queries, keys_all, precision=PRECISE)
    scores = DH ** (-0.5) * low_back(products) + position_bias[None]
    positions = jnp.arange(SEQ, dtype=jnp.int32)
    inside = (positions[None, :] >= starts_group[:, None]) & (positions[None, :] < starts_group[:, None] + PIECE)
    allowed = (positions[:, None] >= positions[None, :])[None] | inside[:, :, None] & inside[:, None, :]
    scores = jnp.where(allowed[:, None], scores, -1e+30)
    weights = low(jax.nn.softmax(scores, axis=-1))
    return jnp.einsum('ghij,gjhd->gihd', weights, values_all, precision=PRECISE)

def slot_tables(routes_block):
    blocks = routes_block.reshape(N_EXPERT, SEQ * TOP)
    onehot = (blocks[:, :, None] == jnp.arange(EXPERTS, dtype=jnp.int32)).astype(jnp.int32)
    earlier = jnp.cumsum(onehot, axis=1) - onehot
    within = lax.optimization_barrier(jnp.sum(earlier * onehot, axis=2))
    source = jnp.arange(N_EXPERT, dtype=jnp.int32)[:, None]
    slot_index = blocks * (N_EXPERT * CAP) + source * CAP + within
    tokens = source * SEQ + jnp.arange(SEQ * TOP, dtype=jnp.int32)[None, :] // TOP
    slot_total = EXPERTS * N_EXPERT * CAP
    owners = jnp.zeros((slot_total,), jnp.int32).at[slot_index.reshape(-1)].set(tokens.reshape(-1))
    filled = jnp.zeros((slot_total,), jnp.float32).at[slot_index.reshape(-1)].set(1.0)
    return (slot_index.reshape(N_EXPERT * SEQ, TOP), owners, filled)

def run_layer(inputs, weights_qkv, weights_out, table_values, gain_pair, weights_first, weights_second, routes_block, gates_block, starts_block, onehot_bias):
    normed = low(rms_norm(inputs, gain_pair[0]))
    projected = jnp.dot(normed, weights_qkv.reshape(D, 3 * HEADS * DH), precision=PRECISE)
    projected = low(low_back(projected)).reshape(N_EXPERT * SEQ, 3, HEADS, DH)
    position_bias = jnp.einsum('ijb,bh->hij', onehot_bias, table_values, precision=PRECISE)
    group_size = math.gcd(N_EXPERT, max(1, 4096 // SEQ))
    grouped = projected.reshape(N_EXPERT // group_size, group_size, SEQ, 3, HEADS, DH)
    starts_grouped = starts_block.reshape(N_EXPERT // group_size, group_size)

    def one_group(group_pair):
        return attend_group(group_pair[0], group_pair[1], position_bias)
    mixed_heads = lax.map(jax.checkpoint(one_group), (grouped, starts_grouped))
    mixed_heads = low(low_back(mixed_heads.reshape(N_EXPERT * SEQ, HEADS * DH)))
    attended = low_back(jnp.dot(mixed_heads, weights_out, precision=PRECISE))
    hidden_state = inputs + attended
    normed_second = low(rms_norm(hidden_state, gain_pair[1]))
    slot_index, owners, filled = slot_tables(routes_block)
    expert_rows = (normed_second[owners] * filled[:, None]).reshape(EXPERTS, N_EXPERT * CAP, D)

    def one_expert(triple):
        hidden_units = low_back(jnp.dot(triple[2], triple[0], precision=PRECISE))
        active = low(jax.nn.gelu(hidden_units))
        return jnp.dot(active, triple[1], precision=PRECISE)
    expert_out = low_back(lax.map(jax.checkpoint(one_expert), (weights_first, weights_second, expert_rows)))
    flat_out = expert_out.reshape(EXPERTS * N_EXPERT * CAP, D)
    picked = flat_out[slot_index]
    combined = lax.optimization_barrier(jnp.sum(gates_block[:, :, None] * picked, axis=1))
    return hidden_state + combined

def reference(inputs, cotangent, qkv_weight, out_weight, rel_bias, norm_gains, first_weight, second_weight, routes, gates, piece_starts):
    onehot_bias = bias_onehot(SEQ)

    def forward(first_inputs, probes, weights_qkv, weights_out, tables, gain_sets, weights_first, weights_second):
        finals = []
        middles = []
        for micro_batch in range(MICRO):
            layer_in = low_back(first_inputs[micro_batch])
            outputs_first = run_layer(layer_in, weights_qkv[0], weights_out[0], tables[0], gain_sets[0], weights_first[0], weights_second[0], routes[0, micro_batch], gates[0, micro_batch], piece_starts[micro_batch], onehot_bias)
            middle = low(outputs_first)
            second_in = low_back(middle + probes[micro_batch])
            outputs_second = run_layer(second_in, weights_qkv[1], weights_out[1], tables[1], gain_sets[1], weights_first[1], weights_second[1], routes[1, micro_batch], gates[1, micro_batch], piece_starts[micro_batch], onehot_bias)
            finals.append(low(outputs_second))
            middles.append(middle)
        return (jnp.stack(finals), jnp.stack(middles))
    finals, pullback, middles = jax.vjp(forward, inputs.astype(jnp.float32), jnp.zeros(inputs.shape, jnp.float32), qkv_weight.astype(jnp.float32), out_weight.astype(jnp.float32), rel_bias.astype(jnp.float32), norm_gains.astype(jnp.float32), first_weight.astype(jnp.float32), second_weight.astype(jnp.float32), has_aux=True)
    gradients = pullback(cotangent.astype(jnp.float32))
    activations = jnp.stack([middles, finals]).astype(jnp.bfloat16)
    input_grads = jnp.stack([gradients[0], gradients[1]]).astype(jnp.bfloat16)
    return (activations, input_grads, gradients[2], gradients[3], gradients[4], gradients[5], gradients[6], gradients[7])
```

```python
import functools

import jax
import jax.numpy as jnp
from jax import lax
from jax.experimental import pallas as pl
from jax.experimental.pallas import tpu as pltpu
from jax.sharding import PartitionSpec as P

DH = 64
NB = 32
PIECE = 256
MICRO = 2
EPSILON = 1e-06
MASKED = -1e30
COST = {
    "attend_forward": 6_300_000_000,
    "attend_backward": 10_400_000_000,
    "experts": 3_900_000_000,
    "grads": 5_000_000_000,
}
LIMIT = 16 << 20
F32 = jnp.float32
BF16 = jnp.bfloat16


def partner(value, axis, flip, name):
    with jax.named_scope(name):
        return lax.ppermute(value, axis, [(i, i ^ flip) for i in range(lax.axis_size(axis))])


def bits_of(size):
    return [1 << b for b in reversed(range(size.bit_length() - 1))]


def spread_tensor(block, name):
    size = lax.axis_size("tensor")
    far_first = [(d, partner(block, "tensor", d, f"{name}_z{d}")) for d in reversed(range(1, size))]
    return [block] + [got for _, got in reversed(far_first)]


def spread_list(value, bits, name):
    chunks = [value]
    for n, bit in enumerate(bits):
        joined = chunks[0] if len(chunks) == 1 else jnp.concatenate(chunks, 0)
        chunks.append(partner(joined, "expert", bit, f"{name}{n}"))
    return chunks


def spread_expert(value, name):
    far_bit, *near_bits = bits_of(lax.axis_size("expert"))
    far = partner(value, "expert", far_bit, f"{name}_far")
    return [
        spread_list(value, near_bits, f"{name}_near"),
        spread_list(far, near_bits, f"{name}_fwd"),
    ]


def relative_ids():
    far_bit, *near_bits = bits_of(lax.axis_size("expert"))
    ids = [0]
    for bit in near_bits:
        ids = ids + [j ^ bit for j in ids]
    return ids, [j ^ far_bit for j in ids]


def fold_list(parts, bits, name):
    parts = list(parts)
    for n, bit in reversed(list(enumerate(bits))):
        got = partner(parts.pop(), "expert", bit, f"{name}{n}")
        start = 0
        for i, part in enumerate(parts):
            count = part.shape[0]
            more = got[start : start + count]
            parts[i] = (part.astype(F32) + more.astype(F32)).astype(BF16)
            start += count
    return parts[0]


def fold_expert(near, far, name):
    far_bit, *near_bits = bits_of(lax.axis_size("expert"))
    far = fold_list(far, near_bits, f"{name}_backfar")
    got = partner(far, "expert", far_bit, f"{name}_backy")
    near = fold_list(near, near_bits, f"{name}_backnear")
    return (near.astype(F32) + got.astype(F32))[0]


def fold_tensor(part, name):
    size = lax.axis_size("tensor")
    rows = part.shape[0] // size
    total = part[:rows]
    low = part.astype(BF16)
    for d in reversed(range(1, size)):
        got = partner(low[d * rows : (d + 1) * rows], "tensor", d, f"{name}_foldz{d}")
        total = total + got.astype(F32)
    return total


def cross_pipe(block, name):
    tensor_size = lax.axis_size("tensor")
    count = 2 * tensor_size
    got = {}
    for d in reversed(range(tensor_size)):
        pairs = [(i, (i ^ tensor_size) ^ d) for i in range(count)]
        with jax.named_scope(f"{name}_x{d}"):
            got[d] = lax.ppermute(block, ("pipe", "tensor"), pairs)
    return [got[d] for d in range(tensor_size)]


def total_expert(value, name):
    for bit in reversed(bits_of(lax.axis_size("expert"))):
        value = value + partner(value, "expert", bit, f"{name}_{bit}")
    return value


def total_halves(values, e, name):
    near_bit, *other_bits = reversed(bits_of(lax.axis_size("expert")))
    side = e % 2
    halves = []
    for n, value in enumerate(values):
        got = partner(value, "expert", near_bit, f"{name}_pair{n}")
        total = value.astype(F32) + got.astype(F32)
        rows = value.shape[0] // 2
        halves.append(lax.dynamic_slice_in_dim(total, side * rows, rows, 0).astype(BF16))
    for bit in other_bits:
        gots = [
            partner(half, "expert", bit, f"{name}_half{n}_{bit}") for n, half in enumerate(halves)
        ]
        halves = [
            (half.astype(F32) + got.astype(F32)).astype(BF16) for half, got in zip(halves, gots)
        ]
    totals = []
    for n, half in enumerate(halves):
        other = partner(half, "expert", near_bit, f"{name}_join{n}")
        low = jnp.where(side == 0, half, other)
        high = jnp.where(side == 0, other, half)
        totals.append(jnp.concatenate([low, high], 0).astype(F32))
    return totals


def bucket_of(offset, bucket_count):
    half_count = bucket_count // 2
    magnitude = jnp.abs(offset)
    octave = jnp.zeros_like(magnitude)
    for exponent in range(1, 13):
        octave = octave + (magnitude >= 2**exponent).astype(jnp.int32)
    inside_bucket = jnp.where(magnitude < 8, magnitude, jnp.minimum(5 + octave, half_count - 1))
    return inside_bucket + half_count * (offset > 0).astype(jnp.int32)


def norm_scale(values):
    return lax.rsqrt(jnp.mean(values * values, axis=-1, keepdims=True) + EPSILON)


def dot(a, b, ca, cb):
    return lax.dot_general(a, b, (((ca,), (cb,)), ((), ())), preferred_element_type=F32)


def whole():
    return pl.BlockSpec(memory_space=pltpu.VMEM)


def scalar():
    return pl.BlockSpec(memory_space=pltpu.SMEM)


def kernel_call(kernel, outs, ins, scalars=0, scratch=(), limit=LIMIT, flops=0, moved=1 << 20):
    return pl.pallas_call(
        kernel,
        out_shape=[jax.ShapeDtypeStruct(s, t) for s, t in outs],
        in_specs=[scalar()] * scalars + [whole()] * (len(ins) - scalars),
        out_specs=[whole()] * len(outs),
        scratch_shapes=[pltpu.VMEM(s, t) for s, t in scratch],
        compiler_params=pltpu.CompilerParams(vmem_limit_bytes=limit),
        cost_estimate=pl.CostEstimate(flops=flops, bytes_accessed=moved, transcendentals=0),
    )(*ins)


def bias_kernel(start_ref, table_ref, bias_ref):
    micros, heads, length, _ = bias_ref.shape
    lanes = -(-2 * length // 128) * 128
    lane = lax.broadcasted_iota(jnp.int32, (8, lanes), 1)
    offset = jnp.where(lane < length, lane, lane - lanes)
    bucket = bucket_of(offset, NB)
    i = lax.broadcasted_iota(jnp.int32, (length, length), 0)
    j = lax.broadcasted_iota(jnp.int32, (length, length), 1)

    def head(h, carry):
        vector = jnp.zeros((8, lanes), F32)
        for b in range(NB):
            vector = jnp.where(bucket == b, table_ref[h, b], vector)
        grid = jnp.broadcast_to(vector[:1], (length, lanes))
        grid = pltpu.roll(grid, 0, 1, stride=1, stride_axis=0)[:, :length]
        for m in range(micros):
            start = start_ref[m]
            inside = (i >= start) & (i < start + PIECE) & (j >= start) & (j < start + PIECE)
            bias_ref[m, h] = jnp.where((j <= i) | inside, grid, MASKED).astype(BF16)
        return carry

    lax.fori_loop(0, heads, head, 0)


def place_blocks(place, block_refs, full_ref):
    rows = block_refs[0].shape[0]
    for d, ref in enumerate(block_refs):
        where = pl.multiple_of((place ^ d) * rows, 8)
        full_ref[pl.ds(where, rows), :] = ref[...].astype(F32)


def lanes_of_half(shape, half):
    lane = lax.broadcasted_iota(jnp.int32, shape, 1)
    return (lane < DH) if half == 0 else (lane >= DH)


def only_half(value, half):
    return jnp.where(lanes_of_half(value.shape, half), value, jnp.zeros_like(value))


def pair_lanes(part, pair, model):
    return pl.ds(pl.multiple_of(part * model + pair * 2 * DH, 2 * DH), 2 * DH)


def attend_forward_kernel(tensor_size, micro, place_ref, *refs):
    blocks = refs[:tensor_size]
    gains_ref, w_ref, wout_ref, bias_ref = refs[tensor_size : tensor_size + 4]
    hidden_ref, own_ref, normed2_ref, normed_ref, qkv_ref, mixed_ref, log_ref = refs[
        tensor_size + 4 : tensor_size + 11
    ]
    x_ref, all_mixed_ref = refs[tensor_size + 11 :]
    place = place_ref[0]
    rows, model = blocks[0].shape
    heads = model // DH
    place_blocks(place, blocks, x_ref)
    x = x_ref[...]
    normed_ref[...] = (x * norm_scale(x) * gains_ref[0:1, :]).astype(BF16)
    for c in range(3):
        for f in range(0, model, 256):
            columns = slice(c * model + f, c * model + f + 256)
            value = dot(normed_ref[...], w_ref[:, columns], 1, 0).astype(BF16)
            if c == 0:
                value = (value * DH**-0.5).astype(BF16)
            qkv_ref[:, columns] = value

    def pair_step(p, carry):
        q, k, v = (qkv_ref[:, pair_lanes(c, p, model)] for c in range(3))
        mixed = None
        for half in range(2):
            scores = dot(only_half(q, half), k, 1, 1) + bias_ref[micro * heads + 2 * p + half].astype(F32)
            top = jnp.max(scores, axis=1, keepdims=True)
            raised = jnp.exp(scores - top)
            total = jnp.sum(raised, axis=1, keepdims=True)
            log_ref[p, :, half : half + 1] = top + jnp.log(total)
            probs = (raised * (1.0 / total)).astype(BF16)
            term = dot(probs, only_half(v, half), 1, 0)
            mixed = term if mixed is None else mixed + term
        all_mixed_ref[:, pair_lanes(0, p, model)] = mixed.astype(BF16)
        return carry

    lax.fori_loop(0, heads // 2, pair_step, 0, unroll=True)
    mixed_ref[...] = all_mixed_ref[:, : mixed_ref.shape[1]]
    for f in range(0, model, 256):
        columns = slice(f, f + 256)
        hidden_ref[:, columns] = x_ref[:, columns] + dot(
            all_mixed_ref[...], wout_ref[:, columns], 1, 0
        )
    hidden = hidden_ref[...]
    normed2_ref[...] = (hidden * norm_scale(hidden) * gains_ref[1:2, :]).astype(BF16)
    own_ref[...] = hidden_ref[pl.ds(pl.multiple_of(place * rows, 8), rows), :]


def attend_forward(place, blocks, weights, gains, bias, m, own_width):
    tensor_size, (rows, model) = len(blocks), blocks[0].shape
    length = rows * tensor_size
    heads = model // DH
    outs = [
        ((length, model), F32),
        ((rows, model), F32),
        ((length, model), BF16),
        ((length, model), BF16),
        ((length, 3 * model), BF16),
        ((length, own_width), BF16),
        ((heads // 2, length, 8), F32),
    ]
    return pl.pallas_call(
        functools.partial(attend_forward_kernel, tensor_size, m),
        out_shape=[jax.ShapeDtypeStruct(s, t) for s, t in outs],
        in_specs=[scalar()] + [whole()] * (tensor_size + 4),
        out_specs=[whole()] * len(outs),
        scratch_shapes=[
            pltpu.VMEM((length, model), F32),
            pltpu.VMEM((length, model), BF16),
        ],
        compiler_params=pltpu.CompilerParams(vmem_limit_bytes=LIMIT),
        cost_estimate=pl.CostEstimate(
            flops=COST["attend_forward"], bytes_accessed=1 << 20, transcendentals=0
        ),
    )(place, *blocks, gains, *weights, bias)


def attend_backward_kernel(tensor_size, micro, place_ref, *refs):
    n = tensor_size
    grads, blocks = refs[:n], refs[n : 2 * n]
    gy_ref, hidden_ref, log_ref, gains_ref = refs[2 * n : 2 * n + 4]
    qkv_ref, w_ref, wout_ref, bias_ref = refs[2 * n + 4 : 2 * n + 8]
    out_ref, own_ref, d_att_ref, d_own_ref, d_scores_ref, gain_ref = refs[2 * n + 8 : 2 * n + 14]
    x_ref, full_ref, d_hidden_ref, d_mixed_ref, d_qkv_ref = refs[2 * n + 14 :]
    place = place_ref[0]
    rows, model = blocks[0].shape
    heads = model // DH
    place_blocks(place, grads, x_ref)
    d_normed2 = x_ref[...]
    hidden = hidden_ref[...]
    s2 = norm_scale(hidden)
    w2 = d_normed2 * gains_ref[1:2, :]
    inner = jnp.mean(w2 * hidden, axis=1, keepdims=True)
    d_hidden = gy_ref[...].astype(F32) + s2 * w2 - hidden * (s2 * s2 * s2 * inner)
    gain_ref[1:2, :] = jnp.sum(d_normed2 * hidden * s2, axis=0, keepdims=True)
    d_hidden_ref[...] = d_hidden
    d_att_ref[...] = d_hidden.astype(BF16)
    for f in range(0, model, 256):
        d_mixed_ref[:, f : f + 256] = dot(d_att_ref[...], wout_ref[f : f + 256, :], 1, 1).astype(
            BF16
        )
    own_heads = d_scores_ref.shape[0]

    def pair_step(p, carry):
        q, k, v = (qkv_ref[:, pair_lanes(c, p, model)] for c in range(3))
        d_mixed = d_mixed_ref[:, pair_lanes(0, p, model)]
        totals = [None, None, None]
        for half in range(2):
            q_half, d_half = only_half(q, half), only_half(d_mixed, half)
            scores = dot(q_half, k, 1, 1) + bias_ref[micro * heads + 2 * p + half].astype(F32)
            probs = jnp.exp(scores - log_ref[p, :, half : half + 1])
            d_probs = dot(d_half, v, 1, 1)
            row = jnp.sum(probs * d_probs, axis=1, keepdims=True)
            d_scores = probs * (d_probs - row)
            low = d_scores.astype(BF16)

            @pl.when(2 * p + half < own_heads)
            def _():
                d_scores_ref[2 * p + half] = d_scores

            terms = (
                dot(low, only_half(k, half), 1, 0),
                dot(low, q_half, 0, 0),
                dot(probs.astype(BF16), d_half, 0, 0),
            )
            totals = [b if a is None else a + b for a, b in zip(totals, terms)]
        d_qkv_ref[:, pair_lanes(0, p, model)] = (totals[0] * DH**-0.5).astype(BF16)
        d_qkv_ref[:, pair_lanes(1, p, model)] = totals[1].astype(BF16)
        d_qkv_ref[:, pair_lanes(2, p, model)] = totals[2].astype(BF16)
        return carry

    lax.fori_loop(0, heads // 2, pair_step, 0, unroll=True)
    width = own_heads * DH
    d_own_ref[...] = jnp.concatenate(
        [d_qkv_ref[:, c * model : c * model + width] for c in range(3)], 1
    )
    d_normed_ref = x_ref
    for f in range(0, model, 256):
        d_normed_ref[:, f : f + 256] = dot(d_qkv_ref[...], w_ref[f : f + 256, :], 1, 1)
    d_normed = d_normed_ref[...]
    place_blocks(place, blocks, full_ref)
    x = full_ref[...]
    s1 = norm_scale(x)
    w1 = d_normed * gains_ref[0:1, :]
    inner = jnp.mean(w1 * x, axis=1, keepdims=True)
    grad = d_hidden_ref[...] + s1 * w1 - x * (s1 * s1 * s1 * inner)
    gain_ref[0:1, :] = jnp.sum(d_normed * x * s1, axis=0, keepdims=True)
    out_ref[...] = grad.astype(BF16)
    d_hidden_ref[...] = grad
    own_ref[...] = d_hidden_ref[pl.ds(pl.multiple_of(place * rows, 8), rows), :].astype(BF16)


def attend_backward(place, grads, blocks, gy, hidden, qkv, logs, weights, gains, bias, m, width):
    tensor_size, (rows, model) = len(blocks), blocks[0].shape
    length = rows * tensor_size
    heads = model // DH
    outs = [
        ((length, model), BF16),
        ((rows, model), BF16),
        ((length, model), BF16),
        ((length, 3 * width), BF16),
        ((width // DH, length, length), F32),
        ((2, model), F32),
    ]
    return pl.pallas_call(
        functools.partial(attend_backward_kernel, tensor_size, m),
        out_shape=[jax.ShapeDtypeStruct(s, t) for s, t in outs],
        in_specs=[scalar()] + [whole()] * (2 * tensor_size + 8),
        out_specs=[whole()] * len(outs),
        scratch_shapes=[
            pltpu.VMEM((length, model), F32),
            pltpu.VMEM((length, model), F32),
            pltpu.VMEM((length, model), F32),
            pltpu.VMEM((length, model), BF16),
            pltpu.VMEM((length, 3 * model), BF16),
        ],
        compiler_params=pltpu.CompilerParams(vmem_limit_bytes=LIMIT),
        cost_estimate=pl.CostEstimate(
            flops=COST["attend_backward"], bytes_accessed=1 << 20, transcendentals=0
        ),
    )(place, *grads, *blocks, gy, hidden, logs, gains, qkv, *weights, bias)


def pick_rows(slot_ref, s, count, length):
    place = lax.broadcasted_iota(jnp.int32, (count, length), 0)
    picked = place == slot_ref[s, 0:1, :]
    for l in range(1, slot_ref.shape[1]):
        picked = picked | (place == slot_ref[s, l : l + 1, :])
    return jnp.where(picked, 1.0, 0.0).astype(BF16)


def slot_gates(slot_ref, gate_ref, s, count, length):
    place = lax.broadcasted_iota(jnp.int32, (count, length), 0)
    value = jnp.zeros((count, length), F32)
    for l in range(slot_ref.shape[1]):
        value = jnp.where(place == slot_ref[s, l : l + 1, :], gate_ref[s, l : l + 1, :], value)
    return jnp.sum(value, axis=1, keepdims=True)


def pick_tokens(turned_ref, s, l, cap, length):
    place = lax.broadcasted_iota(jnp.int32, (length, cap), 1)
    return jnp.where(place == turned_ref[s, :, l : l + 1], 1.0, 0.0).astype(BF16)


def each_sequence(chunk_refs, step):
    base = 0
    for ref in chunk_refs:
        count = ref.shape[0]
        if count == 1:
            step(ref, 0, base)
        else:

            def one(i, carry, ref=ref, base=base):
                step(ref, i, base + i)
                return carry

            lax.fori_loop(0, count, one, 0)
        base += count


def span(s, cap):
    return pl.ds(pl.multiple_of(s * cap, 16), cap)


def scatter_rows(part_refs, turned_ref, rows_ref, cap):
    length = part_refs[0].shape[1]

    def scatter(part_ref, i, s):
        total = None
        for l in range(rows_ref.shape[0]):
            hot = pick_tokens(turned_ref, s, l, cap, length)
            term = dot(hot, rows_ref[l, span(s, cap), :], 1, 0)
            total = term if total is None else total + term
        part_ref[i] = total.astype(BF16)

    each_sequence(part_refs, scatter)


CURVE = 0.7978845608028654
TILE = 256


def experts_forward_kernel(chunks, cap, *refs):
    x_refs = refs[:chunks]
    slot_ref, gate_ref, turned_ref, first_ref, second_ref = refs[chunks : chunks + 5]
    part_refs = refs[chunks + 5 : 2 * chunks + 5]
    rows_ref, active_ref, slope_ref, scaled_ref, weight_ref = refs[2 * chunks + 5 :]
    experts, model, hidden = first_ref.shape
    length = x_refs[0].shape[1]

    def gather(x_ref, i, s):
        rows = dot(pick_rows(slot_ref, s, experts * cap, length), x_ref[i], 1, 0).astype(BF16)
        weight = slot_gates(slot_ref, gate_ref, s, experts * cap, length)
        for l in range(experts):
            rows_ref[l, span(s, cap), :] = rows[l * cap : (l + 1) * cap]
            weight_ref[l, span(s, cap), :] = weight[l * cap : (l + 1) * cap]

    each_sequence(x_refs, gather)
    for l in range(experts):
        for f in range(0, hidden, TILE):
            units = dot(rows_ref[l], first_ref[l, :, f : f + TILE], 1, 0)
            square = units * units
            t = jnp.tanh(units * (CURVE + CURVE * 0.044715 * square))
            half = 0.5 + 0.5 * t
            active_ref[l, :, f : f + TILE] = (units * half).astype(BF16)
            bend = units * (1.0 - t * t) * (0.5 * CURVE + 1.5 * CURVE * 0.044715 * square)
            slope_ref[l, :, f : f + TILE] = (half + bend).astype(BF16)
    for l in range(experts):
        for f in range(0, model, TILE):
            out = dot(active_ref[l], second_ref[l, :, f : f + TILE], 1, 0)
            scaled_ref[l, :, f : f + TILE] = (out * weight_ref[l]).astype(BF16)
    scatter_rows(part_refs, turned_ref, scaled_ref, cap)


def experts_forward(chunks, table, first, second):
    slots, gates, turned, cap = table
    experts, model, hidden = first.shape
    count, length = slots.shape[0], chunks[0].shape[1]
    outs = [(c.shape, BF16) for c in chunks] + [
        ((experts, count * cap, model), BF16),
        ((experts, count * cap, hidden), BF16),
        ((experts, count * cap, hidden), BF16),
    ]
    got = kernel_call(
        functools.partial(experts_forward_kernel, len(chunks), cap),
        outs,
        [*chunks, slots, gates, turned, first, second],
        scratch=[
            ((experts, count * cap, model), BF16),
            ((experts, count * cap, 1), F32),
        ],
        flops=COST["experts"],
        moved=1 << 20,
    )
    return list(got[: len(chunks)]), got[len(chunks) :]


def experts_backward_kernel(chunks, cap, *refs):
    g_refs = refs[:chunks]
    slot_ref, gate_ref, turned_ref, first_ref, second_ref, slope_ref = refs[chunks : chunks + 6]
    part_refs = refs[chunks + 6 : 2 * chunks + 6]
    d_out_ref, d_units_ref, back_ref = refs[2 * chunks + 6 :]
    experts, model, hidden = first_ref.shape
    length = g_refs[0].shape[1]

    def gather(g_ref, i, s):
        rows = dot(pick_rows(slot_ref, s, experts * cap, length), g_ref[i], 1, 0)
        weight = slot_gates(slot_ref, gate_ref, s, experts * cap, length)
        rows = (rows * weight).astype(BF16)
        for l in range(experts):
            d_out_ref[l, span(s, cap), :] = rows[l * cap : (l + 1) * cap]

    each_sequence(g_refs, gather)
    for l in range(experts):
        for f in range(0, hidden, TILE):
            d_active = dot(d_out_ref[l], second_ref[l, f : f + TILE, :], 1, 1)
            d_units_ref[l, :, f : f + TILE] = (
                d_active * slope_ref[l, :, f : f + TILE].astype(F32)
            ).astype(BF16)
    for l in range(experts):
        for f in range(0, model, TILE):
            back_ref[l, :, f : f + TILE] = dot(
                d_units_ref[l], first_ref[l, f : f + TILE, :], 1, 1
            ).astype(BF16)
    scatter_rows(part_refs, turned_ref, back_ref, cap)


def experts_backward(chunks, table, slope, first, second):
    slots, gates, turned, cap = table
    experts, model, hidden = first.shape
    count, length = slots.shape[0], chunks[0].shape[1]
    outs = [(c.shape, BF16) for c in chunks] + [
        ((experts, count * cap, model), BF16),
        ((experts, count * cap, hidden), BF16),
    ]
    got = kernel_call(
        functools.partial(experts_backward_kernel, len(chunks), cap),
        outs,
        [*chunks, slots, gates, turned, first, second, slope],
        scratch=[((experts, count * cap, model), BF16)],
        flops=COST["experts"],
        moved=1 << 20,
    )
    return list(got[: len(chunks)]), got[len(chunks) :]


def weights_kernel(at_ref, own_qkv_ref, own_out_ref, *refs):
    slabs, (qkv_ref, out_ref) = refs[:-2], refs[-2:]
    width, model = own_out_ref.shape
    count = model // width

    def put(rows, d, value):
        for c in range(3):
            columns = slice(c * model + d * width, c * model + (d + 1) * width)
            qkv_ref[rows, columns] = value[:, c * width : (c + 1) * width]

    put(slice(None), 0, own_qkv_ref[...])
    out_ref[:width, :] = own_out_ref[...]
    per = len(slabs) // (count - 1)
    for d in range(1, count):
        index = 0
        for ref in slabs[(d - 1) * per : d * per]:
            for i in range(ref.shape[0]):
                rows = ref.shape[1]
                part = rows // count
                at = at_ref[index]
                put(pl.ds(pl.multiple_of(at * rows, 16), rows), d, ref[i])
                where = pl.ds(pl.multiple_of(d * width + at * part, 16), part)
                for g in range(count):
                    out_ref[where, g * width : (g + 1) * width] = ref[
                        i, g * part : (g + 1) * part, 3 * width :
                    ]
                index += 1


def gather_weights(qkv_weight, out_weight, e, name):
    model = qkv_weight.shape[0]
    width = out_weight.shape[0]
    count = model // width
    expert_size = lax.axis_size("expert")
    own_qkv = qkv_weight.reshape(model, -1)
    slab, part = model // expert_size, width // expert_size
    rows = lax.dynamic_slice_in_dim(own_qkv, e * slab, slab, 0)
    lower = lax.dynamic_slice_in_dim(out_weight, e * part, part, 0)
    lower = lower.reshape(part, count, width).transpose(1, 0, 2).reshape(slab, width)
    mine = jnp.concatenate([rows, lower], 1)[None]
    ids = sum(relative_ids(), [])
    pieces = []
    gots = {d: partner(mine, "tensor", d, f"{name}_z{d}") for d in (1, *reversed(range(2, count)))}
    for d in range(1, count):
        near, far = spread_expert(gots[d], f"{name}{d}")
        pieces.append(near + far)
    if part % 16 == 0:
        with jax.named_scope(f"{name}_join"):
            return kernel_call(
                weights_kernel,
                [((model, 3 * model), BF16), ((model, model), BF16)],
                [e ^ jnp.array(ids, jnp.int32), own_qkv, out_weight, *sum(pieces, [])],
                scalars=1,
            )
    at = jnp.array([ids.index(n) for n in range(expert_size)], jnp.int32)
    places = at[e ^ jnp.arange(expert_size, dtype=jnp.int32)]
    qkv, out = [own_qkv], [out_weight]
    for group in pieces:
        slabs = jnp.take(jnp.concatenate(group, 0), places, axis=0)
        qkv.append(slabs[:, :, : 3 * width].reshape(model, -1))
        lower = slabs[:, :, 3 * width :].reshape(expert_size, count, part, width)
        out.append(lower.transpose(0, 2, 1, 3).reshape(width, model))
    qkv = jnp.stack([q.reshape(model, 3, width) for q in qkv], 2)
    return qkv.reshape(model, 3 * model), jnp.concatenate(out, 0)


def chosen_copy(flag, later_ref, earlier_ref, target_ref, sem):
    @pl.when(flag == 1)
    def _():
        pltpu.make_async_copy(later_ref, target_ref, sem).start()

    @pl.when(flag == 0)
    def _():
        pltpu.make_async_copy(earlier_ref, target_ref, sem).start()

    return pltpu.make_async_copy(later_ref, target_ref, sem)


def expert_grads_kernel(sets, flag_ref, *refs):
    later, earlier = refs[: 2 * sets], refs[2 * sets : 4 * sets]
    out_hbm, left_ref, right_ref, total_ref, in_sems, out_sems = refs[4 * sets :]
    experts, rows = later[0].shape[:2]
    copies = []
    for n in range(2 * sets):
        target = (left_ref, right_ref)[n % 2].at[:, n // 2 * rows : (n // 2 + 1) * rows]
        copies.append(chosen_copy(flag_ref[0], later[n], earlier[n], target, in_sems.at[n]))
    for copy in copies:
        copy.wait()
    done = []
    for l in range(experts):
        for f in range(0, left_ref.shape[2], TILE):
            total_ref[l, f : f + TILE, :] = dot(left_ref[l, :, f : f + TILE], right_ref[l], 0, 0)
            part = pltpu.make_async_copy(
                total_ref.at[l, f : f + TILE], out_hbm.at[l, f : f + TILE], out_sems.at[len(done)]
            )
            part.start()
            done.append(part)
    for part in done:
        part.wait()


def expert_grads(flag, later, earlier):
    sets = len(later)
    left, right = later[0]
    experts, rows = left.shape[:2]
    shape = (experts, left.shape[2], right.shape[2])
    ins = [v for pair in later for v in pair] + [v for pair in earlier for v in pair]
    return pl.pallas_call(
        functools.partial(expert_grads_kernel, sets),
        out_shape=jax.ShapeDtypeStruct(shape, F32),
        in_specs=[scalar()] + [pl.BlockSpec(memory_space=pl.ANY)] * len(ins),
        out_specs=pl.BlockSpec(memory_space=pl.ANY),
        scratch_shapes=[
            pltpu.VMEM((experts, sets * rows, left.shape[2]), BF16),
            pltpu.VMEM((experts, sets * rows, right.shape[2]), BF16),
            pltpu.VMEM(shape, F32),
            pltpu.SemaphoreType.DMA((2 * sets,)),
            pltpu.SemaphoreType.DMA((experts * left.shape[2] // TILE,)),
        ],
        compiler_params=pltpu.CompilerParams(vmem_limit_bytes=24 << 20),
        cost_estimate=pl.CostEstimate(
            flops=COST["grads"], bytes_accessed=1 << 20, transcendentals=0
        ),
    )(flag, *ins)


def attend_grads_kernel(micros, flag_ref, *refs):
    later, earlier = refs[: 4 * micros], refs[4 * micros : 8 * micros]
    qkv_ref, out_ref, *targets, sems = refs[8 * micros :]
    length = later[0].shape[0]
    copies = []
    for n in range(4 * micros):
        target = targets[n % 4].at[n // 4 * length : (n // 4 + 1) * length]
        copies.append(chosen_copy(flag_ref[0], later[n], earlier[n], target, sems.at[n]))
    for copy in copies:
        copy.wait()
    normed_ref, d_qkv_ref, mixed_ref, d_att_ref = targets
    for f in range(0, qkv_ref.shape[0], TILE):
        qkv_ref[f : f + TILE, :] = dot(normed_ref[:, f : f + TILE], d_qkv_ref[...], 0, 0).astype(
            BF16
        )
    out_ref[...] = dot(mixed_ref[...], d_att_ref[...], 0, 0).astype(BF16)


def attend_grads(flag, later, earlier):
    micros = len(later)
    normed, d_qkv, mixed, d_att = later[0]
    length = normed.shape[0]
    ins = [v for group in later for v in group] + [v for group in earlier for v in group]
    return pl.pallas_call(
        functools.partial(attend_grads_kernel, micros),
        out_shape=[
            jax.ShapeDtypeStruct((normed.shape[1], d_qkv.shape[1]), BF16),
            jax.ShapeDtypeStruct((mixed.shape[1], d_att.shape[1]), BF16),
        ],
        in_specs=[scalar()] + [pl.BlockSpec(memory_space=pl.ANY)] * len(ins),
        out_specs=[whole()] * 2,
        scratch_shapes=[pltpu.VMEM((micros * length, v.shape[1]), BF16) for v in later[0]]
        + [pltpu.SemaphoreType.DMA((4 * micros,))],
        compiler_params=pltpu.CompilerParams(vmem_limit_bytes=LIMIT),
        cost_estimate=pl.CostEstimate(
            flops=2_500_000_000, bytes_accessed=1 << 20, transcendentals=0
        ),
    )(flag, *ins)


def small_grads_kernel(micros, flag_ref, *refs):
    later, earlier = refs[: 2 * micros], refs[2 * micros : 4 * micros]
    out_ref, score_ref, gain_ref, sems = refs[4 * micros :]
    copies = []
    for n in range(2 * micros):
        target = (score_ref, gain_ref)[n % 2].at[n // 2]
        copies.append(chosen_copy(flag_ref[0], later[n], earlier[n], target, sems.at[n]))
    for copy in copies:
        copy.wait()
    heads, length = score_ref.shape[1:3]
    lanes = -(-2 * length // 128) * 128
    i = lax.broadcasted_iota(jnp.int32, (length, length), 0)
    j = lax.broadcasted_iota(jnp.int32, (length, length), 1)
    flip = jnp.where(i + j == length - 1, 1.0, 0.0).astype(BF16)
    bucket = bucket_of(lax.broadcasted_iota(jnp.int32, (lanes, 128), 0) - (length - 1), NB)
    onehot = jnp.where(bucket == lax.broadcasted_iota(jnp.int32, (lanes, 128), 1), 1.0, 0.0)
    out_ref[...] = jnp.zeros_like(out_ref)
    gain = gain_ref[0]
    for m in range(1, micros):
        gain = gain + gain_ref[m]
    out_ref[:2, :] = gain
    vectors = []
    for h in range(heads):
        total = score_ref[0, h]
        for m in range(1, micros):
            total = total + score_ref[m, h]
        high = total.astype(BF16)
        low = (total - high.astype(F32)).astype(BF16)
        total = dot(flip, high, 1, 0) + dot(flip, low, 1, 0)
        padded = jnp.concatenate([total, jnp.zeros((length, lanes - length), F32)], 1)
        turned = pltpu.roll(padded, 0, 1, stride=1, stride_axis=0)
        vectors.append(jnp.sum(turned, axis=0, keepdims=True))
    vectors = jnp.concatenate(vectors + [jnp.zeros((8 - heads, lanes), F32)], 0)
    out_ref[8:, :128] = lax.dot_general(
        vectors,
        onehot,
        (((1,), (0,)), ((), ())),
        precision=lax.Precision.HIGHEST,
        preferred_element_type=F32,
    )


def small_grads(flag, later, earlier):
    micros = len(later)
    scores, gain = later[0]
    ins = [v for group in later for v in group] + [v for group in earlier for v in group]
    return pl.pallas_call(
        functools.partial(small_grads_kernel, micros),
        out_shape=jax.ShapeDtypeStruct((16, gain.shape[1]), F32),
        in_specs=[scalar()] + [pl.BlockSpec(memory_space=pl.ANY)] * len(ins),
        out_specs=whole(),
        scratch_shapes=[
            pltpu.VMEM((micros, *scores.shape), F32),
            pltpu.VMEM((micros, *gain.shape), F32),
            pltpu.SemaphoreType.DMA((2 * micros,)),
        ],
        compiler_params=pltpu.CompilerParams(vmem_limit_bytes=LIMIT),
        cost_estimate=pl.CostEstimate(
            flops=2_000_000_000, bytes_accessed=1 << 20, transcendentals=0
        ),
    )(flag, *ins)


def route_tables(routes, gates, e, order, local_experts, capacity):
    ids = e * local_experts + jnp.arange(local_experts, dtype=jnp.int32)
    sent = jnp.concatenate([routes.astype(F32), gates], 2).transpose(0, 2, 1)[None]
    cap = -(-capacity // 16) * 16
    length = routes.shape[1]
    before = jnp.arange(length)[:, None] < jnp.arange(length)[None, :]
    groups = spread_expert(sent, "routes")
    sizes = [sum(v.shape[0] for v in group) for group in groups]
    table = jnp.concatenate(sum(groups, []), 0)
    named, gate = [], []
    for l in range(local_experts):
        hit = table[:, :, :2] == ids[l].astype(F32)
        named.append(jnp.any(hit, axis=2))
        gate.append(jnp.sum(jnp.where(hit, table[:, :, 2:], 0.0), axis=2))
    named, gate = jnp.stack(named, 2), jnp.stack(gate, 2)
    earlier = lax.dot_general(
        named.astype(BF16),
        before.astype(BF16),
        (((3,), (0,)), ((), ())),
        preferred_element_type=F32,
    ).astype(jnp.int32)
    base = jnp.arange(local_experts, dtype=jnp.int32)[:, None] * cap
    slots = jnp.where(named, earlier + base, -1)
    local = jnp.where(named, earlier, -1)
    count = order.shape[0]
    blocks = local.reshape(*local.shape[:3], count, -1)
    blocks = jnp.stack(
        [lax.dynamic_index_in_dim(blocks, order[d], 3, False) for d in range(count)], 3
    )
    turned = blocks.reshape(local.shape).transpose(0, 1, 3, 2)
    tables, start = [], 0
    for size in sizes:
        rows = slice(start, start + size)
        tables.append(
            [(slots[rows, m], gate[rows, m], turned[rows, m], cap) for m in range(MICRO)]
        )
        start += size
    return tables


def body(
    inputs,
    cotangent,
    qkv_weight,
    out_weight,
    rel_bias,
    norm_gains,
    first_weight,
    second_weight,
    routes,
    gates,
    piece_starts,
):
    first_section = lax.axis_index("pipe") == 0
    flag = first_section.astype(jnp.int32)[None]
    z = lax.axis_index("tensor")
    e = lax.axis_index("expert")
    tensor_size = lax.axis_size("tensor")
    expert_size = lax.axis_size("expert")
    rows_here, model_width = inputs.shape[1:]
    length = rows_here * tensor_size
    width = qkv_weight.shape[3]
    own_heads = width // DH
    first, second = first_weight[0], second_weight[0]
    local_experts = first.shape[0]
    capacity = 4 * length // (local_experts * expert_size)
    gains = norm_gains[0].astype(F32)
    place = z.astype(jnp.int32)[None]

    def after(value, token):
        if expert_size <= 4:
            return value
        return lax.optimization_barrier((value, token))[0]

    blocks = [spread_tensor(inputs[m], f"in{m}") for m in range(MICRO)]
    weights = gather_weights(qkv_weight[0], out_weight[0], e, "weights")
    table = jnp.concatenate(spread_tensor(rel_bias[0].T, "table"), 0).astype(F32)
    heads = table.shape[0]
    with jax.named_scope("bias"):
        bias = pl.pallas_call(
            bias_kernel,
            out_shape=jax.ShapeDtypeStruct((MICRO, heads, length, length), BF16),
            in_specs=[scalar(), scalar()],
            out_specs=whole(),
            compiler_params=pltpu.CompilerParams(vmem_limit_bytes=LIMIT),
            cost_estimate=pl.CostEstimate(
                flops=5_000_000_000, bytes_accessed=1 << 20, transcendentals=0
            ),
        )(piece_starts[:, 0], table).reshape(MICRO * heads, length, length)
    order = z ^ jnp.arange(tensor_size, dtype=jnp.int32)
    tables = route_tables(routes[0], gates[0], e, order, local_experts, capacity)

    def layer(blocks, m, tag):
        with jax.named_scope(f"{tag}_attend"):
            hidden, own, normed2, normed, qkv, mixed, logs = attend_forward(
                place, blocks, weights, gains, bias, m, width
            )
        groups, parts, saved = spread_expert(normed2[None], tag), [], []
        for n, (group, table) in enumerate(zip(groups, tables)):
            with jax.named_scope(f"{tag}_experts{n}"):
                part, keep = experts_forward(group, table[m], first, second)
            parts.append(part)
            saved.append(keep)
        total = own + fold_tensor(fold_expert(*parts, tag), tag)
        return total.astype(BF16), (blocks, hidden, normed, qkv, mixed, logs, saved)

    def layer_back(gy, groups, stored, m, tag):
        blocks, hidden, normed, qkv, mixed, logs, saved = stored
        parts, firsts, seconds = [], [], []
        for n, (group, keep, table) in enumerate(zip(groups, saved, tables)):
            rows, active, slope = keep
            with jax.named_scope(f"{tag}_experts{n}"):
                part, (d_out, d_units) = experts_backward(group, table[m], slope, first, second)
            parts.append(part)
            firsts.append((rows, d_units))
            seconds.append((active, d_out))
        own = fold_tensor(fold_expert(*parts, tag), tag).astype(BF16)
        grads = spread_tensor(own, f"{tag}_open")
        with jax.named_scope(f"{tag}_attend"):
            grad_in, own_grad, d_att, d_qkv, d_scores, gain = attend_backward(
                place, grads, blocks, gy, hidden, qkv, logs, weights, gains, bias, m, width
            )
        kept = (firsts, seconds, (normed, d_qkv, mixed, d_att), (d_scores, gain))
        return grad_in, own_grad, kept

    outs, stores = [], []
    for step in range(2):
        outs.append([])
        stores.append([])
        for m in range(MICRO):
            entering = after(blocks[m], outs[step][-1:])
            out, stored = layer(entering, m, f"f{step}m{m}")
            outs[step].append(out)
            stores[step].append(stored)
        if step == 0:
            blocks = [cross_pipe(outs[0][m], f"f0m{m}") for m in range(MICRO)]

    gys = []
    for m in range(MICRO):
        got = jnp.stack(spread_tensor(after(cotangent[m], outs[1]), f"cot{m}"))
        ordered = [lax.dynamic_index_in_dim(got, order[d], 0, False) for d in range(tensor_size)]
        gys.append(jnp.concatenate(ordered, 0))
    grads, kepts = [], []
    for step in range(2):
        results = []
        for m in range(MICRO):
            gy = after(gys[m], [r[0] for r in results])
            tag = f"b{step}m{m}"
            groups = spread_expert(gy[None], tag)
            results.append(layer_back(gy, groups, stores[1 - step][m], m, tag))
        grads.append([r[1] for r in results])
        kepts.append([r[2] for r in results])
        if step == 0:
            gys = [partner(results[m][0], "pipe", 1, f"b0m{m}_hop") for m in range(MICRO)]

    activations = jnp.stack(
        [jnp.where(first_section, outs[0][m], outs[1][m]) for m in range(MICRO)]
    )
    input_grads = jnp.stack(
        [jnp.where(first_section, grads[1][m], grads[0][m]) for m in range(MICRO)]
    )

    def sets(step, n):
        return [pair for kept in kepts[step] for pair in kept[n]]

    with jax.named_scope("second_grad"):
        second_grad = expert_grads(flag, sets(1, 1), sets(0, 1))
    with jax.named_scope("first_grad"):
        first_grad = expert_grads(flag, sets(1, 0), sets(0, 0))
    with jax.named_scope("attend_grads"):
        sums = attend_grads(flag, [k[2] for k in kepts[1]], [k[2] for k in kepts[0]])
    qkv_total, out_total = total_halves(sums, e, "total")
    with jax.named_scope("small_grads"):
        small = small_grads(flag, [k[3] for k in kepts[1]], [k[3] for k in kepts[0]])
    small = total_expert(small, "small")
    return (
        activations[None],
        input_grads[None],
        qkv_total.reshape(qkv_weight.shape),
        out_total[None],
        small[8 : 8 + own_heads, :NB].T[None],
        small[None, :2],
        first_grad[None],
        second_grad[None],
    )


def solution(mesh):
    return jax.shard_map(
        body,
        mesh=mesh,
        in_specs=(
            P(None, ("expert", "tensor"), None),
            P(None, ("expert", "tensor"), None),
            P("pipe", None, None, "tensor"),
            P("pipe", "tensor", None),
            P("pipe", None, "tensor"),
            P("pipe", None, None),
            P("pipe", "expert", None, "tensor"),
            P("pipe", "expert", "tensor", None),
            P("pipe", None, "expert", None),
            P("pipe", None, "expert", None),
            P(None, "expert"),
        ),
        out_specs=(
            P("pipe", None, ("expert", "tensor"), None),
            P("pipe", None, ("expert", "tensor"), None),
            P("pipe", None, None, "tensor"),
            P("pipe", "tensor", None),
            P("pipe", None, "tensor"),
            P("pipe", None, None),
            P("pipe", "expert", None, "tensor"),
            P("pipe", "expert", "tensor", None),
        ),
        check_vma=False,
    )
```
